256 devices in a mesh: row: 32 (over x, z), col: 8 (over y, core).
Axes of the slice: x: 4, y: 4, z: 8, core: 2. Of those that a mesh axis runs over, the one named last changes fastest.
Arguments:
- mom_a: float32 [1536, 12288], P('row', 'col'), may hold values from -6 to 6
- grad_a: float32 [1536, 12288], P('row', 'col'), may hold values from -6 to 6
- basis_a: float32 [512, 12288], P('row', 'col'), may hold values from -0.0546875 to 0.0546875
- mom_b: float32 [7168, 1536], P('row', 'col'), may hold values from -6 to 6
- grad_b: float32 [7168, 1536], P('row', 'col'), may hold values from -6 to 6
- basis_b: float32 [512, 1536], P('row', 'col'), may hold values from -0.15625 to 0.15625
Outputs:
- new_mom_a: float32 [1536, 12288], P('row', 'col')
- update_a: bfloat16 [1536, 12288], P('row', 'col')
- new_basis_a: float32 [512, 12288], P('row', 'col')
- new_mom_b: float32 [7168, 1536], P('row', 'col')
- update_b: bfloat16 [7168, 1536], P('row', 'col')
- new_basis_b: float32 [512, 1536], P('row', 'col')
The draws below stay inside these ranges and needn't reach their ends.
All inputs are finite; a program needn't handle non-finite values.
Results may differ from the reference program's by a relative error of at most 0.0049.
Values sent between devices are 32-bit elements; how exact they have to be, the bound alone decides.
No kernel may reach another device: no remote copies, remote signals or barrier semaphores. Data moves between devices by JAX's collectives and lax.ppermute only.
A program may use at most 64 MiB of HBM per device.

```python
import math
import jax
import jax.numpy as jnp
from jax import lax

M_A = 1536
N_A = 12288
M_B = 7168
N_B = 1536
RANK = 512


def strong_factors(key, offset, row_count, col_count):
    strong_rank = 3 * RANK // 4
    left_factor = jax.random.normal(jax.random.fold_in(key, offset + 1), (row_count, strong_rank), jnp.float32) / math.sqrt(row_count)
    right_factor = jax.random.normal(jax.random.fold_in(key, offset + 2), (strong_rank, col_count), jnp.float32) / math.sqrt(col_count)
    low_end = 1.0
    high_end = 5.0
    strength = jnp.exp(jax.random.uniform(jax.random.fold_in(key, offset + 3), (strong_rank,), jnp.float32, math.log(low_end), math.log(high_end)))
    ratios = jax.random.uniform(jax.random.fold_in(key, offset + 4), (strong_rank,), jnp.float32, 0.5, 1.5)
    amplitude = 0.2 * math.sqrt(row_count * col_count / RANK)
    return (left_factor * amplitude, right_factor, strength, ratios)


def noise_field(key, offset, row_count, col_count):
    noise_term = jax.random.normal(key_mix(key, offset), (row_count, col_count), jnp.float32)
    return 0.2 * noise_term


def key_mix(key, offset):
    return jax.random.fold_in(key, offset)


def draw_matrix(key, offset, row_count, col_count, second):
    left_factor, right_factor, strength, ratios = strong_factors(key, offset, row_count, col_count)
    if second:
        weights = strength * ratios
        noise_offset = offset + 20
    else:
        weights = strength
        noise_offset = offset + 10
    low_rank = jnp.dot(left_factor * weights[None, :], right_factor, precision=lax.Precision.HIGHEST, preferred_element_type=jnp.float32)
    noise_term = noise_field(key, noise_offset, row_count, col_count)
    return jnp.clip(low_rank + noise_term, -6.0, 6.0)


def draw_mom_a(key, part):
    return draw_matrix(key, 100, M_A, N_A, False)


def draw_grad_a(key, part):
    return draw_matrix(key, 100, M_A, N_A, True)


def draw_mom_b(key, part):
    return draw_matrix(key, 200, M_B, N_B, False)


def draw_grad_b(key, part):
    return draw_matrix(key, 200, M_B, N_B, True)


def levels(stream_key, shape, pieces, low, largest):
    def one(position, blocks):
        heights = jax.random.uniform(jax.random.fold_in(jax.random.fold_in(stream_key, 6), position), (blocks,), jnp.float32, low / len(pieces), largest / len(pieces))
        return jnp.repeat(jnp.exp(heights), shape[position] // blocks).reshape((-1,) + (1,) * (len(shape) - position - 1))

    factor_of = one(*pieces[0])
    for cut in pieces[1:]:
        factor_of = factor_of * one(*cut)
    return factor_of


def bell_draw(rng, dims, width, limit, split=(), held_as=jnp.bfloat16):
    values = jax.random.normal(rng, dims, jnp.float32) * width
    if len(split) > 0:
        values = levels(rng, dims, split, -0.22, 0.18) * values
    return jnp.clip(values, min=-limit, max=limit).astype(held_as)


def setup_inputs(seed: int = 0) -> dict:
    keys = jax.random.split(jax.random.key(seed), 7)
    return {
        "mom_a": draw_mom_a(jax.random.fold_in(keys[6], 71), 0),
        "grad_a": draw_grad_a(jax.random.fold_in(keys[6], 71), 0),
        "basis_a": bell_draw(keys[2], (RANK, N_A), N_A ** -0.5, 0.0546875, ((0, 32), (1, 8)), jnp.float32),
        "mom_b": draw_mom_b(jax.random.fold_in(keys[6], 71), 0),
        "grad_b": draw_grad_b(jax.random.fold_in(keys[6], 71), 0),
        "basis_b": bell_draw(keys[5], (RANK, N_B), N_B ** -0.5, 0.15625, ((0, 32), (1, 8)), jnp.float32),
    }


MU = 0.95
EPS = 1e-06

def dion_step(mom, grad, basis):
    highest = lax.Precision.HIGHEST
    buffer = MU * mom + grad
    proj = jnp.dot(buffer.astype(jnp.float32), basis.T.astype(jnp.float32), precision=highest, preferred_element_type=jnp.float32)
    gram = jnp.dot(proj.T.astype(jnp.float32), proj.astype(jnp.float32), precision=highest, preferred_element_type=jnp.float32)
    lower = jnp.linalg.cholesky(gram)
    ortho = lax.linalg.triangular_solve(lower, proj, left_side=False, lower=True, transpose_a=True)
    trans = jnp.dot(ortho.T.astype(jnp.float32), buffer.astype(jnp.float32), precision=highest, preferred_element_type=jnp.float32)
    new_mom = buffer - (1.0 - MU) * jnp.dot(ortho.astype(jnp.float32), trans.astype(jnp.float32), precision=highest, preferred_element_type=jnp.float32)
    norms = jnp.sqrt(lax.optimization_barrier(jnp.sum(trans * trans, axis=1, keepdims=True)) + EPS)
    new_basis = trans / norms
    scale = math.sqrt(buffer.shape[0] * buffer.shape[1] / basis.shape[0])
    update = (jnp.dot(ortho.astype(jnp.float32), new_basis.astype(jnp.float32), precision=highest, preferred_element_type=jnp.float32) * scale).astype(jnp.bfloat16)
    return (new_mom, update, new_basis)

def reference(mom_a, grad_a, basis_a, mom_b, grad_b, basis_b):
    first = dion_step(mom_a, grad_a, basis_a)
    second = dion_step(mom_b, grad_b, basis_b)
    return (first[0], first[1], first[2], second[0], second[1], second[2])
```

```python
import functools
import math

import jax
import jax.numpy as jnp
from jax import lax
from jax.experimental import pallas as pl
from jax.experimental.pallas import tpu as pltpu
from jax.sharding import Mesh
from jax.sharding import PartitionSpec as P

MU = 0.95
EPS = 1e-06
TILE = 128
STRIP = 16
HIGHEST = lax.Precision.HIGHEST


def contract(a, b, ca, cb):
    return lax.dot_general(
        a, b, (((ca,), (cb,)), ((), ())), precision=HIGHEST, preferred_element_type=jnp.float32
    )


def eliminated(rows, first):
    sub = lax.broadcasted_iota(jnp.int32, (STRIP, TILE), 0)
    cols = [
        jnp.broadcast_to(rows[:, first + j : first + j + 1], (STRIP, TILE)) for j in range(STRIP)
    ]
    left, right = rows[:, :TILE], rows[:, TILE:]
    pivots = jnp.zeros((STRIP, TILE), jnp.float32)
    for j in range(STRIP):
        pivot = jnp.broadcast_to(cols[j][j : j + 1, :], (STRIP, TILE))
        pivots = jnp.where(sub == j, pivot, pivots)
        if j == STRIP - 1:
            break
        factor = jnp.where(sub > j, cols[j], 0.0) * (1.0 / pivot)
        for k in range(j + 1, STRIP):
            cols[k] = cols[k] - factor * jnp.broadcast_to(cols[k][j : j + 1, :], (STRIP, TILE))
        left = left - factor * jnp.broadcast_to(left[j : j + 1, :], (STRIP, TILE))
        right = right - factor * jnp.broadcast_to(right[j : j + 1, :], (STRIP, TILE))
    scale = lax.rsqrt(pivots)
    return left * scale, right * scale


def inverse_factor_kernel(gram_ref, inv_ref, work_ref, tile_ref):
    size = gram_ref.shape[0]
    work_ref[...] = gram_ref[...]
    inv_ref[...] = jnp.zeros_like(inv_ref)
    eye = (
        lax.broadcasted_iota(jnp.int32, (TILE, TILE), 0)
        == lax.broadcasted_iota(jnp.int32, (TILE, TILE), 1)
    ).astype(jnp.float32)
    for k in range(size // TILE):
        lo, hi = k * TILE, (k + 1) * TILE
        tile_ref[:, :TILE] = work_ref[lo:hi, lo:hi]
        tile_ref[:, TILE:] = eye
        for top in range(0, TILE, STRIP):
            end = top + STRIP
            left, right = eliminated(tile_ref[top:end, :], top)
            tile_ref[top:end, TILE:] = right
            if end < TILE:
                both = jnp.concatenate([left, right], axis=1)
                tile_ref[end:, :] = tile_ref[end:, :] - contract(left, both, 0, 0)[end:, :]
        own = tile_ref[:, TILE:]
        if k:
            inv_ref[lo:hi, :lo] = contract(own, inv_ref[lo:hi, :lo], 1, 0)
        inv_ref[lo:hi, lo:hi] = own
        if hi < size:
            below = contract(work_ref[hi:, lo:hi], own, 1, 1)
            work_ref[hi:, hi:] = work_ref[hi:, hi:] - contract(below, below, 1, 1)
            inv_ref[hi:, :hi] = inv_ref[hi:, :hi] - contract(below, inv_ref[lo:hi, :hi], 1, 0)


def inverse_factor(gram):
    size = gram.shape[0]
    return pl.pallas_call(
        inverse_factor_kernel,
        out_shape=jax.ShapeDtypeStruct((size, size), jnp.float32),
        in_specs=[pl.BlockSpec(memory_space=pltpu.VMEM)],
        out_specs=pl.BlockSpec(memory_space=pltpu.VMEM),
        scratch_shapes=[
            pltpu.VMEM((size, size), jnp.float32),
            pltpu.VMEM((TILE, 2 * TILE), jnp.float32),
        ],
        compiler_params=pltpu.CompilerParams(vmem_limit_bytes=24 << 20),
        cost_estimate=pl.CostEstimate(
            flops=20_000_000_000, bytes_accessed=2 << 20, transcendentals=512
        ),
        name="inverse_factor",
    )(gram)


def swapped(parts, axes):
    return lax.all_to_all(parts, axes, 0, 0, tiled=True)


def sent_to_all(array, axes):
    size = math.prod(lax.axis_size(a) for a in (axes if isinstance(axes, tuple) else (axes,)))
    return swapped(jnp.broadcast_to(array[None], (size, *array.shape)), axes)


ROW = ("x", "z")
COL = ("y", "core")


def shards(mom_a, grad_a, basis_a, mom_b, grad_b, basis_b):
    nx, nz, ny, nc = (lax.axis_size(a) for a in ("x", "z", "y", "core"))
    ix, iz, iy, ic = (lax.axis_index(a) for a in ("x", "z", "y", "core"))
    nrow, ncol = nx * nz, ny * nc
    rows_a, cols_a = mom_a.shape
    rows_b, cols_b = mom_b.shape
    own = basis_a.shape[0]
    rank = own * nrow
    part_a = cols_a // nx

    with jax.named_scope("buffers"):
        buf_b = MU * mom_b + grad_b
        both = jnp.concatenate([MU * mom_a + grad_a, basis_a], axis=0)
        both = both.reshape(rows_a + own, nx, part_a).transpose(1, 0, 2)
    with jax.named_scope("relayout_a"):
        both = swapped(both, "x")
        buf_a = both[:, :rows_a].reshape(nx * rows_a, part_a)
        bas_a = both[:, rows_a:].reshape(nx * own, part_a)
    with jax.named_scope("gather_basis_b"):
        full_b = sent_to_all(basis_b, ROW).reshape(rank, cols_b)
    with jax.named_scope("gather_basis_a"):
        full_a = sent_to_all(bas_a, "z")
        full_a = full_a.reshape(nz, nx, own, part_a).transpose(1, 0, 2, 3).reshape(rank, part_a)

    with jax.named_scope("project"):
        proj_a = contract(buf_a, full_a, 1, 1)
        proj_b = contract(buf_b, full_b, 1, 1)
        some_a = proj_a.shape[0] // ncol
        some_b = proj_b.shape[0] // ncol
        mixed = jnp.concatenate(
            [proj_a.reshape(ncol, some_a, rank), proj_b.reshape(ncol, some_b, rank)], axis=1
        )
        mixed = jnp.sum(swapped(mixed, COL), axis=0)
        sum_a = jnp.sum(sent_to_all(mixed[:some_a], "x"), axis=0)
        mixed = sent_to_all(jnp.concatenate([sum_a, mixed[some_a:]], axis=0), COL)
        proj_a = mixed[:, :some_a].reshape(ncol * some_a, rank)
        proj_b = mixed[:, some_a:].reshape(ncol * some_b, rank)

    with jax.named_scope("gram"):
        mine = lax.dynamic_slice_in_dim(proj_a, ix * rows_a, rows_a, 0)
        mine = jnp.pad(mine, ((0, rows_b - rows_a), (0, 0)))
        chosen = jnp.where(ic == 0, mine, proj_b)
        band = rank // ny
        left = lax.dynamic_slice_in_dim(chosen, iy * band, band, 1)
        piece = contract(left, chosen, 0, 0)
        piece = jnp.sum(swapped(piece.reshape(nrow, band // nrow, rank), ROW), axis=0)
        piece = sent_to_all(piece, ROW).reshape(band, rank)
        gram = sent_to_all(piece, "y").reshape(rank, rank)

    with jax.named_scope("products"):
        w_a = contract(proj_a, buf_a, 0, 0)
        w_b = contract(proj_b, buf_b, 0, 0)
        w_a = lax.psum_scatter(w_a, "z", scatter_dimension=0, tiled=True)
        w_b = jnp.sum(swapped(w_b.reshape(nrow, own, cols_b), ROW), axis=0)
        w_a = sent_to_all(w_a, "z").reshape(rank, part_a)
        w_b = sent_to_all(w_b, ROW).reshape(rank, cols_b)

    with jax.named_scope("factor"):
        inv = inverse_factor(gram)
        invs = sent_to_all(inv, "core")
        inv_a, inv_b = invs[0], invs[1]

    with jax.named_scope("finish"):
        ortho_a = contract(proj_a, inv_a, 1, 1)
        ortho_b = contract(proj_b, inv_b, 1, 1)
        trans_a = contract(inv_a, w_a, 1, 0)
        trans_b = contract(inv_b, w_b, 1, 0)
        squares = jnp.stack([jnp.sum(trans_a * trans_a, axis=1), jnp.sum(trans_b * trans_b, axis=1)])
        squares = sent_to_all(squares, ("x", "y", "core")).reshape(nx, ncol, 2, rank)
        sq_a = jnp.sum(squares[:, :, 0], axis=(0, 1))
        sq_b = jnp.sum(lax.dynamic_index_in_dim(squares[:, :, 1], ix, 0, keepdims=False), axis=0)
        norms_a = jnp.sqrt(sq_a + EPS)[:, None]
        norms_b = jnp.sqrt(sq_b + EPS)[:, None]
        basis_new_a = trans_a / norms_a
        basis_new_b = trans_b / norms_b
        scale_a = math.sqrt(rows_a * nrow * cols_a * ncol / rank)
        scale_b = math.sqrt(rows_b * nrow * cols_b * ncol / rank)
        mom_new_a = buf_a - (1.0 - MU) * contract(ortho_a, trans_a, 1, 0)
        mom_new_b = buf_b - (1.0 - MU) * contract(ortho_b, trans_b, 1, 0)
        upd_a = contract(ortho_a, basis_new_a, 1, 0) * scale_a
        upd_b = contract(ortho_b, basis_new_b, 1, 0) * scale_b
        out_b = lax.dynamic_slice_in_dim(basis_new_b, (ix * nz + iz) * own, own, 0)

    with jax.named_scope("relayout_out"):
        shares = lax.dynamic_index_in_dim(
            basis_new_a.reshape(nx, nz, own, part_a), iz, 1, keepdims=False
        )
        late = jnp.concatenate(
            [
                mom_new_a.reshape(nx, rows_a, part_a),
                upd_a.reshape(nx, rows_a, part_a),
                shares,
            ],
            axis=1,
        )
        late = swapped(late, "x")
        late = late.transpose(1, 0, 2).reshape(2 * rows_a + own, cols_a)
    return (
        late[:rows_a],
        late[rows_a : 2 * rows_a].astype(jnp.bfloat16),
        late[2 * rows_a :],
        mom_new_b,
        upd_b.astype(jnp.bfloat16),
        out_b,
    )


def solution(mesh):
    fine = Mesh(mesh.devices.reshape(4, 8, 4, 2), ("x", "z", "y", "core"))
    spec = P(ROW, COL)
    return jax.shard_map(
        shards, mesh=fine, in_specs=(spec,) * 6, out_specs=(spec,) * 6, check_vma=False
    )
```

```python
import functools
import math

import jax
import jax.numpy as jnp
from jax import lax
from jax.experimental import pallas as pl
from jax.experimental.pallas import tpu as pltpu
from jax.sharding import Mesh
from jax.sharding import PartitionSpec as P

MU = 0.95
EPS = 1e-06
TILE = 128
STRIP = 16
HIGHEST = lax.Precision.HIGHEST


def contract(a, b, ca, cb):
    return lax.dot_general(
        a, b, (((ca,), (cb,)), ((), ())), precision=HIGHEST, preferred_element_type=jnp.float32
    )


def eliminated(rows, first):
    sub = lax.broadcasted_iota(jnp.int32, (STRIP, TILE), 0)
    cols = [
        jnp.broadcast_to(rows[:, first + j : first + j + 1], (STRIP, TILE)) for j in range(STRIP)
    ]
    left, right = rows[:, :TILE], rows[:, TILE:]
    pivots = jnp.zeros((STRIP, TILE), jnp.float32)
    for j in range(STRIP):
        pivot = jnp.broadcast_to(cols[j][j : j + 1, :], (STRIP, TILE))
        pivots = jnp.where(sub == j, pivot, pivots)
        if j == STRIP - 1:
            break
        factor = jnp.where(sub > j, cols[j], 0.0) * (1.0 / pivot)
        for k in range(j + 1, STRIP):
            cols[k] = cols[k] - factor * jnp.broadcast_to(cols[k][j : j + 1, :], (STRIP, TILE))
        left = left - factor * jnp.broadcast_to(left[j : j + 1, :], (STRIP, TILE))
        right = right - factor * jnp.broadcast_to(right[j : j + 1, :], (STRIP, TILE))
    scale = lax.rsqrt(pivots)
    return left * scale, right * scale


def inverse_factor_kernel(place_ref, *refs):
    *band_refs, inv_ref, work_ref, tile_ref = refs
    size = inv_ref.shape[0]
    band, count = band_refs[0].shape[0], len(band_refs)
    for k, band_ref in enumerate(band_refs):
        at = pl.multiple_of(lax.rem(place_ref[0] + k, count) * band, band)
        work_ref[pl.ds(at, band), :] = band_ref[...]
    inv_ref[...] = jnp.zeros_like(inv_ref)
    eye = (
        lax.broadcasted_iota(jnp.int32, (TILE, TILE), 0)
        == lax.broadcasted_iota(jnp.int32, (TILE, TILE), 1)
    ).astype(jnp.float32)
    for k in range(size // TILE):
        lo, hi = k * TILE, (k + 1) * TILE
        tile_ref[:, :TILE] = work_ref[lo:hi, lo:hi]
        tile_ref[:, TILE:] = eye
        for top in range(0, TILE, STRIP):
            end = top + STRIP
            left, right = eliminated(tile_ref[top:end, :], top)
            tile_ref[top:end, TILE:] = right
            if end < TILE:
                both = jnp.concatenate([left, right], axis=1)
                tile_ref[end:, :] = tile_ref[end:, :] - contract(left, both, 0, 0)[end:, :]
        own = tile_ref[:, TILE:]
        if k:
            inv_ref[lo:hi, :lo] = contract(own, inv_ref[lo:hi, :lo], 1, 0)
        inv_ref[lo:hi, lo:hi] = own
        if hi < size:
            below = contract(work_ref[hi:, lo:hi], own, 1, 1)
            work_ref[hi:, hi:] = work_ref[hi:, hi:] - contract(below, below, 1, 1)
            inv_ref[hi:, :hi] = inv_ref[hi:, :hi] - contract(below, inv_ref[lo:hi, :hi], 1, 0)


def inverse_factor(bands, place):
    size = bands[0].shape[1]
    return pl.pallas_call(
        inverse_factor_kernel,
        out_shape=jax.ShapeDtypeStruct((size, size), jnp.float32),
        in_specs=[pl.BlockSpec(memory_space=pltpu.SMEM)]
        + [pl.BlockSpec(memory_space=pltpu.VMEM)] * len(bands),
        out_specs=pl.BlockSpec(memory_space=pltpu.VMEM),
        scratch_shapes=[
            pltpu.VMEM((size, size), jnp.float32),
            pltpu.VMEM((TILE, 2 * TILE), jnp.float32),
        ],
        compiler_params=pltpu.CompilerParams(vmem_limit_bytes=24 << 20),
        cost_estimate=pl.CostEstimate(
            flops=20_000_000_000, bytes_accessed=2 << 20, transcendentals=512
        ),
        name="inverse_factor",
    )(jnp.full((1,), place, jnp.int32), *bands)


def swapped(parts, axes):
    return lax.all_to_all(parts, axes, 0, 0, tiled=True)


def sent_to_all(array, axes):
    size = math.prod(lax.axis_size(a) for a in (axes if isinstance(axes, tuple) else (axes,)))
    return swapped(jnp.broadcast_to(array[None], (size, *array.shape)), axes)


def from_ahead(array, axis, step):
    size = lax.axis_size(axis)
    return lax.ppermute(array, axis, [((i + step) % size, i) for i in range(size)])


def summed_around(array, axis):
    return array + sum(from_ahead(array, axis, k) for k in range(1, lax.axis_size(axis)))


def around(array, axis):
    return [array] + [from_ahead(array, axis, k) for k in range(1, lax.axis_size(axis))]


def in_order(blocks, axis):
    size = len(blocks)
    start = lax.rem(size - lax.axis_index(axis), size)
    return lax.dynamic_slice_in_dim(jnp.stack(blocks + blocks[: size - 1]), start, size, 0)


def summed_exchange(parts, axis):
    size = lax.axis_size(axis)
    index = lax.axis_index(axis)
    total = lax.dynamic_index_in_dim(parts, index, 0, keepdims=False)
    for k in range(1, size):
        sent = lax.dynamic_index_in_dim(parts, lax.rem(index + size - k, size), 0, keepdims=False)
        total = total + from_ahead(sent, axis, k)
    return total


def exchanged_around(parts, axis):
    size = lax.axis_size(axis)
    index = lax.axis_index(axis)
    blocks = []
    for k in range(size):
        sent = lax.dynamic_index_in_dim(parts, lax.rem(index + size - k, size), 0, keepdims=False)
        blocks.append(from_ahead(sent, axis, k) if k else sent)
    return in_order(blocks, axis)


ROW = ("x", "z")
COL = ("y", "core")


def shards(mom_a, grad_a, basis_a, mom_b, grad_b, basis_b):
    nx, nz, ny, nc = (lax.axis_size(a) for a in ("x", "z", "y", "core"))
    ix, iz, iy, ic = (lax.axis_index(a) for a in ("x", "z", "y", "core"))
    nrow, ncol = nx * nz, ny * nc
    rows_a, cols_a = mom_a.shape
    rows_b, cols_b = mom_b.shape
    own = basis_a.shape[0]
    rank = own * nrow
    part_a = cols_a // nx

    with jax.named_scope("buffers"):
        buf_b = MU * mom_b + grad_b
        both = jnp.concatenate([MU * mom_a + grad_a, basis_a], axis=0)
        both = both.reshape(rows_a + own, nx, part_a).transpose(1, 0, 2)
    with jax.named_scope("relayout_a"):
        bas_b = sent_to_all(basis_b, "z").reshape(nz * own, cols_b)
        both = exchanged_around(both, "x")
        bas_b, both = lax.optimization_barrier((bas_b, both))
        buf_a = both[:, :rows_a].reshape(nx * rows_a, part_a)
        bas_a = both[:, rows_a:].reshape(nx * own, part_a)
    with jax.named_scope("gather_bases"):
        full_b = in_order(around(bas_b, "x"), "x").reshape(rank, cols_b)
        proj_b = contract(buf_b, full_b, 1, 1)
        full_a = sent_to_all(bas_a, "z").reshape(nz, nx, own, part_a)
        full_a = full_a.transpose(1, 0, 2, 3).reshape(rank, part_a)
        full_a, proj_b = lax.optimization_barrier((full_a, proj_b))

    with jax.named_scope("project"):
        proj_a = contract(buf_a, full_a, 1, 1)
        half_a, half_b = proj_a.shape[0] // nc, proj_b.shape[0] // nc
        some_a, some_b = half_a // ny, half_b // ny
        mixed = jnp.concatenate(
            [proj_a.reshape(nc, ny, some_a, rank), proj_b.reshape(nc, ny, some_b, rank)], axis=2
        )
        mixed = jnp.sum(swapped(mixed, "core"), axis=0)
        mixed = jnp.sum(swapped(mixed, "y"), axis=0)
        sum_a = summed_around(mixed[:some_a], "x")
        mixed = sent_to_all(jnp.concatenate([sum_a, mixed[some_a:]], axis=0), "y")
        mixed = lax.all_gather(mixed, "core", axis=0)
        proj_a = mixed[:, :, :some_a].reshape(nc * half_a, rank)
        proj_b = mixed[:, :, some_a:].reshape(nc * half_b, rank)

    with jax.named_scope("gram"):
        w_a = contract(proj_a, buf_a, 0, 0)
        mine = lax.dynamic_slice_in_dim(proj_a, ix * rows_a, rows_a, 0)
        mine = jnp.pad(mine, ((0, rows_b - rows_a), (0, 0)))
        chosen = jnp.where(ic == 0, mine, proj_b)
        band = rank // ny
        left = lax.dynamic_slice_in_dim(chosen, iy * band, band, 1)
        piece = contract(left, chosen, 0, 0).reshape(nrow, band // nrow, rank)
        w_b = contract(proj_b, buf_b, 0, 0).reshape(nx, rank // nx, cols_b)
        w_b = summed_exchange(w_b, "x").reshape(nz, 2, own // 2, cols_b)
        w_b = jnp.concatenate([w_b[:, 0], w_b[:, 1]], axis=2)
        w_ab = jnp.concatenate([w_a.reshape(nz, rank // nz, part_a), w_b], axis=1)
        piece = jnp.sum(swapped(piece, ROW), axis=0)
        piece, w_ab = lax.optimization_barrier((sent_to_all(piece, ROW), w_ab))
        bands = around(piece.reshape(band, rank), "y")
        w_ab = jnp.sum(swapped(w_ab, "z"), axis=0)
        bands, w_ab = lax.optimization_barrier((bands, w_ab))
        w_ab = sent_to_all(w_ab, "z")

    with jax.named_scope("factor"):
        inv, w_ab = lax.optimization_barrier((inverse_factor(bands, iy), w_ab))
        w_a = w_ab[:, : rank // nz].reshape(rank, part_a)
        w_b = w_ab[:, rank // nz :]
        w_b = jnp.stack([w_b[:, :, :cols_b], w_b[:, :, cols_b:]], axis=1).reshape(nz * own, cols_b)
        w_b = in_order(around(w_b, "x"), "x").reshape(rank, cols_b)
        other = from_ahead(inv, "core", 1)
        inv_a = jnp.where(ic == 0, inv, other)
        inv_b = jnp.where(ic == 0, other, inv)

    with jax.named_scope("finish"):
        ortho_a = contract(proj_a, inv_a, 1, 1)
        ortho_b = contract(proj_b, inv_b, 1, 1)
        trans_a = contract(inv_a, w_a, 1, 0)
        trans_b = contract(inv_b, w_b, 1, 0)
        squares = jnp.stack([jnp.sum(trans_a * trans_a, axis=1), jnp.sum(trans_b * trans_b, axis=1)])
        squares = sent_to_all(squares, ("x", "y", "core")).reshape(nx, ncol, 2, rank)
        sq_a = jnp.sum(squares[:, :, 0], axis=(0, 1))
        sq_b = jnp.sum(lax.dynamic_index_in_dim(squares[:, :, 1], ix, 0, keepdims=False), axis=0)
        norms_a = jnp.sqrt(sq_a + EPS)[:, None]
        norms_b = jnp.sqrt(sq_b + EPS)[:, None]
        basis_new_a = trans_a / norms_a
        basis_new_b = trans_b / norms_b
        scale_a = math.sqrt(rows_a * nrow * cols_a * ncol / rank)
        scale_b = math.sqrt(rows_b * nrow * cols_b * ncol / rank)
        mom_new_a = buf_a - (1.0 - MU) * contract(ortho_a, trans_a, 1, 0)
        mom_new_b = buf_b - (1.0 - MU) * contract(ortho_b, trans_b, 1, 0)
        upd_a = contract(ortho_a, basis_new_a, 1, 0) * scale_a
        upd_b = contract(ortho_b, basis_new_b, 1, 0) * scale_b
        out_b = lax.dynamic_slice_in_dim(basis_new_b, (ix * nz + iz) * own, own, 0)

    with jax.named_scope("relayout_out"):
        shares = lax.dynamic_index_in_dim(
            basis_new_a.reshape(nx, nz, own, part_a), iz, 1, keepdims=False
        )
        late = jnp.concatenate(
            [
                mom_new_a.reshape(nx, rows_a, part_a),
                upd_a.reshape(nx, rows_a, part_a),
                shares,
            ],
            axis=1,
        )
        late = swapped(late, "x")
        late = late.transpose(1, 0, 2).reshape(2 * rows_a + own, cols_a)
    return (
        late[:rows_a],
        late[rows_a : 2 * rows_a].astype(jnp.bfloat16),
        late[2 * rows_a :],
        mom_new_b,
        upd_b.astype(jnp.bfloat16),
        out_b,
    )


def solution(mesh):
    fine = Mesh(mesh.devices.reshape(4, 8, 4, 2), ("x", "z", "y", "core"))
    spec = P(ROW, COL)
    return jax.shard_map(
        shards, mesh=fine, in_specs=(spec,) * 6, out_specs=(spec,) * 6, check_vma=False
    )
```

```python
import functools
import math

import jax
import jax.numpy as jnp
from jax import lax
from jax.experimental import pallas as pl
from jax.experimental.pallas import tpu as pltpu
from jax.sharding import Mesh
from jax.sharding import PartitionSpec as P

MU = 0.95
EPS = 1e-06
TILE = 128
STRIP = 32
HIGHEST = lax.Precision.HIGHEST
HIGH = lax.Precision.HIGH


def contract(a, b, ca, cb, precision=HIGHEST):
    return lax.dot_general(
        a, b, (((ca,), (cb,)), ((), ())), precision=precision, preferred_element_type=jnp.float32
    )


def eliminated(rows, first):
    sub = lax.broadcasted_iota(jnp.int32, (STRIP, TILE), 0)
    cols = [
        jnp.broadcast_to(rows[:, first + j : first + j + 1], (STRIP, TILE)) for j in range(STRIP)
    ]
    left, right = rows[:, :TILE], rows[:, TILE:]
    pivots = jnp.zeros((STRIP, TILE), jnp.float32)
    for j in range(STRIP):
        pivot = jnp.broadcast_to(cols[j][j : j + 1, :], (STRIP, TILE))
        pivots = jnp.where(sub == j, pivot, pivots)
        if j == STRIP - 1:
            break
        factor = jnp.where(sub > j, cols[j], 0.0) * (1.0 / pivot)
        for k in range(j + 1, STRIP):
            cols[k] = cols[k] - factor * jnp.broadcast_to(cols[k][j : j + 1, :], (STRIP, TILE))
        left = left - factor * jnp.broadcast_to(left[j : j + 1, :], (STRIP, TILE))
        right = right - factor * jnp.broadcast_to(right[j : j + 1, :], (STRIP, TILE))
    scale = lax.rsqrt(pivots)
    return left * scale, right * scale


def inverse_factor_kernel(place_ref, *refs):
    *band_refs, inv_ref, work_ref, tile_ref = refs
    size = inv_ref.shape[0]
    band, count = band_refs[0].shape[0], len(band_refs)
    for k, band_ref in enumerate(band_refs):
        at = pl.multiple_of(lax.rem(place_ref[0] + k, count) * band, band)
        work_ref[pl.ds(at, band), :] = band_ref[...]
    inv_ref[...] = jnp.zeros_like(inv_ref)
    eye = (
        lax.broadcasted_iota(jnp.int32, (TILE, TILE), 0)
        == lax.broadcasted_iota(jnp.int32, (TILE, TILE), 1)
    ).astype(jnp.float32)
    for k in range(size // TILE):
        lo, hi = k * TILE, (k + 1) * TILE
        tile_ref[:, :TILE] = work_ref[lo:hi, lo:hi]
        tile_ref[:, TILE:] = eye
        for top in range(0, TILE, STRIP):
            end = top + STRIP
            left, right = eliminated(tile_ref[top:end, :], top)
            tile_ref[top:end, TILE:] = right
            if end < TILE:
                both = jnp.concatenate([left, right], axis=1)
                tile_ref[end:, :] = tile_ref[end:, :] - contract(left, both, 0, 0)[end:, :]
        own = tile_ref[:, TILE:]
        if k:
            inv_ref[lo:hi, :lo] = contract(own, inv_ref[lo:hi, :lo], 1, 0)
        inv_ref[lo:hi, lo:hi] = own
        if hi < size:
            below = contract(work_ref[hi:, lo:hi], own, 1, 1)
            work_ref[hi:, hi:] = work_ref[hi:, hi:] - contract(below, below, 1, 1)
            inv_ref[hi:, :hi] = inv_ref[hi:, :hi] - contract(below, inv_ref[lo:hi, :hi], 1, 0)


def inverse_factor(bands, place):
    size = bands[0].shape[1]
    return pl.pallas_call(
        inverse_factor_kernel,
        out_shape=jax.ShapeDtypeStruct((size, size), jnp.float32),
        in_specs=[pl.BlockSpec(memory_space=pltpu.SMEM)]
        + [pl.BlockSpec(memory_space=pltpu.VMEM)] * len(bands),
        out_specs=pl.BlockSpec(memory_space=pltpu.VMEM),
        scratch_shapes=[
            pltpu.VMEM((size, size), jnp.float32),
            pltpu.VMEM((TILE, 2 * TILE), jnp.float32),
        ],
        compiler_params=pltpu.CompilerParams(vmem_limit_bytes=24 << 20),
        cost_estimate=pl.CostEstimate(
            flops=20_000_000_000, bytes_accessed=2 << 20, transcendentals=512
        ),
        name="inverse_factor",
    )(jnp.full((1,), place, jnp.int32), *bands)


def swapped(parts, axes):
    return lax.all_to_all(parts, axes, 0, 0, tiled=True)


def sent_to_all(array, axes):
    size = math.prod(lax.axis_size(a) for a in (axes if isinstance(axes, tuple) else (axes,)))
    return swapped(jnp.broadcast_to(array[None], (size, *array.shape)), axes)


def from_ahead(array, axis, step):
    size = lax.axis_size(axis)
    return lax.ppermute(array, axis, [((i + step) % size, i) for i in range(size)])


def summed_around(array, axis):
    return array + sum(from_ahead(array, axis, k) for k in range(1, lax.axis_size(axis)))


def around(array, axis):
    return [array] + [from_ahead(array, axis, k) for k in range(1, lax.axis_size(axis))]


def place_kernel(first_ref, *refs):
    *block_refs, out_ref = refs
    for k, block_ref in enumerate(block_refs):
        out_ref[lax.rem(first_ref[0] + k, len(block_refs))] = block_ref[...]


def in_order(blocks, axis):
    shape = blocks[0].shape
    return pl.pallas_call(
        place_kernel,
        out_shape=jax.ShapeDtypeStruct((len(blocks), *shape), jnp.float32),
        in_specs=[pl.BlockSpec(memory_space=pltpu.SMEM)]
        + [pl.BlockSpec(memory_space=pltpu.VMEM)] * len(blocks),
        out_specs=pl.BlockSpec(memory_space=pltpu.VMEM),
        cost_estimate=pl.CostEstimate(
            flops=0, bytes_accessed=8 * len(blocks) * math.prod(shape), transcendentals=0
        ),
        compiler_params=pltpu.CompilerParams(vmem_limit_bytes=8 << 20),
        name="in_order",
    )(jnp.full((1,), lax.axis_index(axis), jnp.int32), *blocks)


def summed_exchange(parts, axis):
    size = lax.axis_size(axis)
    index = lax.axis_index(axis)
    total = lax.dynamic_index_in_dim(parts, index, 0, keepdims=False)
    for k in range(1, size):
        sent = lax.dynamic_index_in_dim(parts, lax.rem(index + size - k, size), 0, keepdims=False)
        total = total + from_ahead(sent, axis, k)
    return total


def exchanged_around(parts, axis):
    size = lax.axis_size(axis)
    index = lax.axis_index(axis)
    blocks = []
    for k in range(size):
        sent = lax.dynamic_index_in_dim(parts, lax.rem(index + size - k, size), 0, keepdims=False)
        blocks.append(from_ahead(sent, axis, k) if k else sent)
    return in_order(blocks, axis)


ROW = ("x", "z")
COL = ("y", "core")


def shards(mom_a, grad_a, basis_a, mom_b, grad_b, basis_b):
    nx, nz, ny, nc = (lax.axis_size(a) for a in ("x", "z", "y", "core"))
    ix, iz, iy, ic = (lax.axis_index(a) for a in ("x", "z", "y", "core"))
    nrow, ncol = nx * nz, ny * nc
    rows_a, cols_a = mom_a.shape
    rows_b, cols_b = mom_b.shape
    own = basis_a.shape[0]
    rank = own * nrow
    part_a = cols_a // nx

    with jax.named_scope("buffers"):
        buf_b = MU * mom_b + grad_b
        both = jnp.concatenate([MU * mom_a + grad_a, basis_a], axis=0)
        both = both.reshape(rows_a + own, nx, part_a).transpose(1, 0, 2)
    with jax.named_scope("relayout_a"):
        bas_b = sent_to_all(basis_b, "z").reshape(nz * own, cols_b)
        both = exchanged_around(both, "x")
        bas_b, both = lax.optimization_barrier((bas_b, both))
        buf_a = both[:, :rows_a].reshape(nx * rows_a, part_a)
        bas_a = both[:, rows_a:].reshape(nx * own, part_a)
    with jax.named_scope("gather_bases"):
        full_b = in_order(around(bas_b, "x"), "x").reshape(rank, cols_b)
        proj_b = contract(buf_b, full_b, 1, 1)
        full_a = sent_to_all(bas_a, "z").reshape(nz, nx, own, part_a)
        full_a = full_a.transpose(1, 0, 2, 3).reshape(rank, part_a)
        full_a, proj_b = lax.optimization_barrier((full_a, proj_b))

    with jax.named_scope("project"):
        proj_a = contract(buf_a, full_a, 1, 1)
        half_a, half_b = proj_a.shape[0] // nc, proj_b.shape[0] // nc
        some_a, some_b = half_a // ny, half_b // ny
        mixed = jnp.concatenate(
            [proj_a.reshape(nc, ny, some_a, rank), proj_b.reshape(nc, ny, some_b, rank)], axis=2
        )
        mixed = jnp.sum(swapped(mixed, "core"), axis=0)
        mixed = summed_exchange(mixed, "y")
        sum_a = summed_around(mixed[:some_a], "x")
        mixed = around(jnp.concatenate([sum_a, mixed[some_a:]], axis=0), "y")
        mixed = lax.all_gather(jnp.stack(mixed), "core", axis=0)
        ring_a = mixed[:, :, :some_a].reshape(nc * half_a, rank)
        ring_b = mixed[:, :, some_a:].reshape(nc * half_b, rank)
        mixed = in_order([mixed[:, k] for k in range(ny)], "y")
        proj_a = mixed[:, :, :some_a].transpose(1, 0, 2, 3).reshape(nc * half_a, rank)
        proj_b = mixed[:, :, some_a:].transpose(1, 0, 2, 3).reshape(nc * half_b, rank)

    with jax.named_scope("gram"):
        w_a = contract(proj_a, buf_a, 0, 0)
        mine = lax.dynamic_slice_in_dim(ring_a, ix * rows_a, rows_a, 0)
        mine = jnp.pad(mine, ((0, rows_b - rows_a), (0, 0)))
        chosen = jnp.where(ic == 0, mine, ring_b)
        band = rank // ny
        left = lax.dynamic_slice_in_dim(chosen, iy * band, band, 1)
        piece = contract(left, chosen, 0, 0).reshape(nrow, band // nrow, rank)
        w_b = contract(buf_b, proj_b, 0, 0).reshape(nx, cols_b // nx, rank)
        w_b = summed_exchange(w_b, "x").reshape(nz, cols_b * rank // nrow // part_a, part_a)
        w_ab = jnp.concatenate([w_a.reshape(nz, rank // nz, part_a), w_b], axis=1)
        piece = jnp.sum(swapped(piece, ROW), axis=0)
        piece, w_ab = lax.optimization_barrier((sent_to_all(piece, ROW), w_ab))
        bands = around(piece.reshape(band, rank), "y")
        w_ab = jnp.sum(swapped(w_ab, "z"), axis=0)
        bands, w_ab = lax.optimization_barrier((bands, w_ab))
        w_ab = sent_to_all(w_ab, "z")

    with jax.named_scope("factor"):
        inv, w_ab = lax.optimization_barrier((inverse_factor(bands, iy), w_ab))
        w_a = w_ab[:, : rank // nz].reshape(rank, part_a)
        w_b = w_ab[:, rank // nz :].reshape(cols_b // nx, rank)
        other = from_ahead(inv, "core", 1)
        inv_a = jnp.where(ic == 0, inv, other)
        inv_b = jnp.where(ic == 0, other, inv)

    with jax.named_scope("finish"):
        trans_a = contract(inv_a, w_a, 1, 0, HIGH)
        trans_b = contract(w_b, inv_b, 1, 1, HIGH)
        squares = jnp.stack([jnp.sum(trans_a * trans_a, axis=1), jnp.sum(trans_b * trans_b, axis=0)])
        squares, proj_a, proj_b, trans_b = lax.optimization_barrier(
            (squares, proj_a, proj_b, trans_b)
        )
        norms = jnp.sqrt(jnp.sum(sent_to_all(squares, ("x", "y", "core")), axis=0) + EPS)
        ortho_a = contract(proj_a, inv_a, 1, 1, HIGH)
        ortho_b = contract(proj_b, inv_b, 1, 1, HIGH)
        trans_b = in_order(around(trans_b, "x"), "x").reshape(cols_b, rank)
        basis_new_a = trans_a / norms[0][:, None]
        basis_new_b = trans_b / norms[1][None, :]
        scale_a = math.sqrt(rows_a * nrow * cols_a * ncol / rank)
        scale_b = math.sqrt(rows_b * nrow * cols_b * ncol / rank)
        mom_new_a = buf_a - (1.0 - MU) * contract(ortho_a, trans_a, 1, 0, HIGH)
        mom_new_b = buf_b - (1.0 - MU) * contract(ortho_b, trans_b, 1, 1, HIGH)
        upd_a = contract(ortho_a, basis_new_a, 1, 0, HIGH) * scale_a
        upd_b = contract(ortho_b, basis_new_b, 1, 1, HIGH) * scale_b
        out_b = lax.dynamic_slice_in_dim(basis_new_b, (ix * nz + iz) * own, own, 1).T

    with jax.named_scope("relayout_out"):
        shares = lax.dynamic_index_in_dim(
            basis_new_a.reshape(nx, nz, own, part_a), iz, 1, keepdims=False
        )
        late = jnp.concatenate(
            [
                mom_new_a.reshape(nx, rows_a, part_a),
                upd_a.reshape(nx, rows_a, part_a),
                shares,
            ],
            axis=1,
        )
        late = swapped(late, "x").transpose(1, 0, 2).reshape(2 * rows_a + own, cols_a)
    return (
        late[:rows_a],
        late[rows_a : 2 * rows_a].astype(jnp.bfloat16),
        late[2 * rows_a :],
        mom_new_b,
        upd_b.astype(jnp.bfloat16),
        out_b,
    )


def solution(mesh):
    fine = Mesh(mesh.devices.reshape(4, 8, 4, 2), ("x", "z", "y", "core"))
    spec = P(ROW, COL)
    return jax.shard_map(
        shards, mesh=fine, in_specs=(spec,) * 6, out_specs=(spec,) * 6, check_vma=False
    )
```

```python
import functools
import math

import jax
import jax.numpy as jnp
from jax import lax
from jax.experimental import pallas as pl
from jax.experimental.pallas import tpu as pltpu
from jax.sharding import Mesh
from jax.sharding import PartitionSpec as P

MU = 0.95
EPS = 1e-06
TILE = 128
STRIP = 32
HIGHEST = lax.Precision.HIGHEST
HIGH = lax.Precision.HIGH


def contract(a, b, ca, cb, precision=HIGHEST):
    return lax.dot_general(
        a, b, (((ca,), (cb,)), ((), ())), precision=precision, preferred_element_type=jnp.float32
    )


def eliminated(rows, first):
    sub = lax.broadcasted_iota(jnp.int32, (STRIP, TILE), 0)
    cols = [
        jnp.broadcast_to(rows[:, first + j : first + j + 1], (STRIP, TILE)) for j in range(STRIP)
    ]
    left, right = rows[:, :TILE], rows[:, TILE:]
    pivots = jnp.zeros((STRIP, TILE), jnp.float32)
    for j in range(STRIP):
        pivot = jnp.broadcast_to(cols[j][j : j + 1, :], (STRIP, TILE))
        pivots = jnp.where(sub == j, pivot, pivots)
        if j == STRIP - 1:
            break
        factor = jnp.where(sub > j, cols[j], 0.0) * (1.0 / pivot)
        for k in range(j + 1, STRIP):
            cols[k] = cols[k] - factor * jnp.broadcast_to(cols[k][j : j + 1, :], (STRIP, TILE))
        left = left - factor * jnp.broadcast_to(left[j : j + 1, :], (STRIP, TILE))
        right = right - factor * jnp.broadcast_to(right[j : j + 1, :], (STRIP, TILE))
    scale = lax.rsqrt(pivots)
    return left * scale, right * scale


def inverse_factor_kernel(place_ref, *refs):
    *band_refs, inv_ref, work_ref, tile_ref = refs
    size = inv_ref.shape[0]
    band, count = band_refs[0].shape[0], len(band_refs)
    for k, band_ref in enumerate(band_refs):
        at = pl.multiple_of(lax.rem(place_ref[0] + k, count) * band, band)
        work_ref[pl.ds(at, band), :] = band_ref[...]
    inv_ref[...] = jnp.zeros_like(inv_ref)
    eye = (
        lax.broadcasted_iota(jnp.int32, (TILE, TILE), 0)
        == lax.broadcasted_iota(jnp.int32, (TILE, TILE), 1)
    ).astype(jnp.float32)
    for k in range(size // TILE):
        lo, hi = k * TILE, (k + 1) * TILE
        tile_ref[:, :TILE] = work_ref[lo:hi, lo:hi]
        tile_ref[:, TILE:] = eye
        for top in range(0, TILE, STRIP):
            end = top + STRIP
            left, right = eliminated(tile_ref[top:end, :], top)
            tile_ref[top:end, TILE:] = right
            if end < TILE:
                both = jnp.concatenate([left, right], axis=1)
                tile_ref[end:, :] = tile_ref[end:, :] - contract(left, both, 0, 0)[end:, :]
        own = tile_ref[:, TILE:]
        if k:
            inv_ref[lo:hi, :lo] = contract(own, inv_ref[lo:hi, :lo], 1, 0)
        inv_ref[lo:hi, lo:hi] = own
        if hi < size:
            below = contract(work_ref[hi:, lo:hi], own, 1, 1)
            work_ref[hi:, hi:] = work_ref[hi:, hi:] - contract(below, below, 1, 1)
            inv_ref[hi:, :hi] = inv_ref[hi:, :hi] - contract(below, inv_ref[lo:hi, :hi], 1, 0)


def inverse_factor(bands, place):
    size = bands[0].shape[1]
    return pl.pallas_call(
        inverse_factor_kernel,
        out_shape=jax.ShapeDtypeStruct((size, size), jnp.float32),
        in_specs=[pl.BlockSpec(memory_space=pltpu.SMEM)]
        + [pl.BlockSpec(memory_space=pltpu.VMEM)] * len(bands),
        out_specs=pl.BlockSpec(memory_space=pltpu.VMEM),
        scratch_shapes=[
            pltpu.VMEM((size, size), jnp.float32),
            pltpu.VMEM((TILE, 2 * TILE), jnp.float32),
        ],
        compiler_params=pltpu.CompilerParams(vmem_limit_bytes=24 << 20),
        cost_estimate=pl.CostEstimate(
            flops=20_000_000_000, bytes_accessed=2 << 20, transcendentals=512
        ),
        name="inverse_factor",
    )(jnp.full((1,), place, jnp.int32), *bands)


def swapped(parts, axes):
    return lax.all_to_all(parts, axes, 0, 0, tiled=True)


def sent_to_all(array, axes):
    size = math.prod(lax.axis_size(a) for a in (axes if isinstance(axes, tuple) else (axes,)))
    return swapped(jnp.broadcast_to(array[None], (size, *array.shape)), axes)


def from_ahead(array, axis, step):
    size = lax.axis_size(axis)
    return lax.ppermute(array, axis, [((i + step) % size, i) for i in range(size)])


def summed_around(array, axis):
    return array + sum(from_ahead(array, axis, k) for k in range(1, lax.axis_size(axis)))


def around(array, axis):
    return [array] + [from_ahead(array, axis, k) for k in range(1, lax.axis_size(axis))]


def place_kernel(first_ref, *refs):
    *block_refs, out_ref = refs
    for k, block_ref in enumerate(block_refs):
        out_ref[lax.rem(first_ref[0] + k, len(block_refs))] = block_ref[...]


def in_order(blocks, axis):
    shape = blocks[0].shape
    return pl.pallas_call(
        place_kernel,
        out_shape=jax.ShapeDtypeStruct((len(blocks), *shape), jnp.float32),
        in_specs=[pl.BlockSpec(memory_space=pltpu.SMEM)]
        + [pl.BlockSpec(memory_space=pltpu.VMEM)] * len(blocks),
        out_specs=pl.BlockSpec(memory_space=pltpu.VMEM),
        cost_estimate=pl.CostEstimate(
            flops=0, bytes_accessed=8 * len(blocks) * math.prod(shape), transcendentals=0
        ),
        compiler_params=pltpu.CompilerParams(vmem_limit_bytes=8 << 20),
        name="in_order",
    )(jnp.full((1,), lax.axis_index(axis), jnp.int32), *blocks)


def summed_exchange(parts, axis):
    size = lax.axis_size(axis)
    index = lax.axis_index(axis)
    total = lax.dynamic_index_in_dim(parts, index, 0, keepdims=False)
    for k in range(1, size):
        sent = lax.dynamic_index_in_dim(parts, lax.rem(index + size - k, size), 0, keepdims=False)
        total = total + from_ahead(sent, axis, k)
    return total


def exchanged_around(parts, axis):
    size = lax.axis_size(axis)
    index = lax.axis_index(axis)
    blocks = []
    for k in range(size):
        sent = lax.dynamic_index_in_dim(parts, lax.rem(index + size - k, size), 0, keepdims=False)
        blocks.append(from_ahead(sent, axis, k) if k else sent)
    return in_order(blocks, axis)


ROW = ("x", "z")
COL = ("y", "core")


def shards(mom_a, grad_a, basis_a, mom_b, grad_b, basis_b):
    nx, nz, ny, nc = (lax.axis_size(a) for a in ("x", "z", "y", "core"))
    ix, iz, iy, ic = (lax.axis_index(a) for a in ("x", "z", "y", "core"))
    nrow, ncol = nx * nz, ny * nc
    rows_a, cols_a = mom_a.shape
    rows_b, cols_b = mom_b.shape
    own = basis_a.shape[0]
    rank = own * nrow
    part_a = cols_a // nx

    with jax.named_scope("buffers"):
        buf_b = MU * mom_b + grad_b
        both = jnp.concatenate([MU * mom_a + grad_a, basis_a], axis=0)
        both = both.reshape(rows_a + own, nx, part_a).transpose(1, 0, 2)
    with jax.named_scope("relayout_a"):
        bas_b = sent_to_all(basis_b, "z").reshape(nz * own, cols_b)
        both = exchanged_around(both, "x")
        bas_b, both = lax.optimization_barrier((bas_b, both))
        buf_a = both[:, :rows_a].reshape(nx * rows_a, part_a)
        bas_a = both[:, rows_a:].reshape(nx * own, part_a)
    with jax.named_scope("gather_bases"):
        full_b = in_order(around(bas_b, "x"), "x").reshape(rank, cols_b)
        proj_b = contract(buf_b, full_b, 1, 1)
        full_a = sent_to_all(bas_a, "z").reshape(nz, nx, own, part_a)
        full_a = full_a.transpose(1, 0, 2, 3).reshape(rank, part_a)
        full_a, proj_b = lax.optimization_barrier((full_a, proj_b))

    with jax.named_scope("project"):
        proj_a = contract(buf_a, full_a, 1, 1)
        half_a, half_b = proj_a.shape[0] // nc, proj_b.shape[0] // nc
        some_a, some_b = half_a // ny, half_b // ny
        mixed = jnp.concatenate(
            [proj_a.reshape(nc, ny, some_a, rank), proj_b.reshape(nc, ny, some_b, rank)], axis=2
        )
        mixed = jnp.sum(swapped(mixed, "core"), axis=0)
        mixed = summed_exchange(mixed, "y")
        sum_a = summed_around(mixed[:some_a], "x")
        mixed = around(jnp.concatenate([sum_a, mixed[some_a:]], axis=0), "y")
        mixed = lax.all_gather(jnp.stack(mixed), "core", axis=0)
        ring_a = mixed[:, :, :some_a].reshape(nc * half_a, rank)
        ring_b = mixed[:, :, some_a:].reshape(nc * half_b, rank)
        mixed = in_order([mixed[:, k] for k in range(ny)], "y")
        proj_a = mixed[:, :, :some_a].transpose(1, 0, 2, 3).reshape(nc * half_a, rank)
        proj_b = mixed[:, :, some_a:].transpose(1, 0, 2, 3).reshape(nc * half_b, rank)

    with jax.named_scope("gram"):
        w_a = contract(proj_a, buf_a, 0, 0)
        mine = lax.dynamic_slice_in_dim(ring_a, ix * rows_a, rows_a, 0)
        mine = jnp.pad(mine, ((0, rows_b - rows_a), (0, 0)))
        chosen = jnp.where(ic == 0, mine, ring_b)
        band = rank // ny
        left = lax.dynamic_slice_in_dim(chosen, iy * band, band, 1)
        piece = contract(left, chosen, 0, 0).reshape(nrow, band // nrow, rank)
        w_b = contract(buf_b, proj_b, 0, 0).reshape(nx, cols_b // nx, rank)
        w_b = summed_exchange(w_b, "x").reshape(-1, 8, rank // TILE, TILE).transpose(0, 2, 1, 3)
        w_b = w_b.reshape(nz, -1, 8, TILE).transpose(0, 2, 1, 3).reshape(nz, 8, part_a)
        w_ab = jnp.concatenate([w_a.reshape(nz, rank // nz, part_a), w_b], axis=1)
        piece = jnp.sum(swapped(piece, ROW), axis=0)
        piece, w_ab = lax.optimization_barrier((sent_to_all(piece, ROW), w_ab))
        bands = around(piece.reshape(band, rank), "y")
        w_ab = jnp.sum(swapped(w_ab, "z"), axis=0)
        bands, w_ab = lax.optimization_barrier((bands, w_ab))
        w_ab = sent_to_all(w_ab, "z")

    with jax.named_scope("factor"):
        inv, w_ab = lax.optimization_barrier((inverse_factor(bands, iy), w_ab))
        w_a = w_ab[:, : rank // nz].reshape(rank, part_a)
        w_b = w_ab[:, rank // nz :].reshape(nz, 8, -1, TILE).transpose(0, 2, 1, 3)
        w_b = w_b.reshape(-1, rank // TILE, 8, TILE).transpose(0, 2, 1, 3)
        w_b = w_b.reshape(cols_b // nx, rank)
        other = from_ahead(inv, "core", 1)
        inv_a = jnp.where(ic == 0, inv, other)
        inv_b = jnp.where(ic == 0, other, inv)

    with jax.named_scope("finish"):
        trans_a = contract(inv_a, w_a, 1, 0, HIGH)
        trans_b = contract(w_b, inv_b, 1, 1, HIGH)
        squares = jnp.stack([jnp.sum(trans_a * trans_a, axis=1), jnp.sum(trans_b * trans_b, axis=0)])
        squares, proj_a, proj_b, trans_b = lax.optimization_barrier(
            (squares, proj_a, proj_b, trans_b)
        )
        norms = jnp.sqrt(jnp.sum(sent_to_all(squares, ("x", "y", "core")), axis=0) + EPS)
        ortho_a = contract(proj_a, inv_a, 1, 1, HIGH)
        ortho_b = contract(proj_b, inv_b, 1, 1, HIGH)
        trans_b = in_order(around(trans_b, "x"), "x").reshape(cols_b, rank)
        basis_new_a = trans_a / norms[0][:, None]
        basis_new_b = trans_b / norms[1][None, :]
        scale_a = math.sqrt(rows_a * nrow * cols_a * ncol / rank)
        scale_b = math.sqrt(rows_b * nrow * cols_b * ncol / rank)
        mom_new_a = buf_a - (1.0 - MU) * contract(ortho_a, trans_a, 1, 0, HIGH)
        mom_new_b = buf_b - (1.0 - MU) * contract(ortho_b, trans_b, 1, 1, HIGH)
        upd_a = contract(ortho_a, basis_new_a, 1, 0, HIGH) * scale_a
        upd_b = contract(ortho_b, basis_new_b, 1, 1, HIGH) * scale_b
        out_b = lax.dynamic_slice_in_dim(basis_new_b, (ix * nz + iz) * own, own, 1).T

    with jax.named_scope("relayout_out"):
        shares = lax.dynamic_index_in_dim(
            basis_new_a.reshape(nx, nz, own, part_a), iz, 1, keepdims=False
        )
        late = jnp.concatenate(
            [
                mom_new_a.reshape(nx, rows_a, part_a),
                upd_a.reshape(nx, rows_a, part_a),
                shares,
            ],
            axis=1,
        )
        late = swapped(late, "x").transpose(1, 0, 2).reshape(2 * rows_a + own, cols_a)
    return (
        late[:rows_a],
        late[rows_a : 2 * rows_a].astype(jnp.bfloat16),
        late[2 * rows_a :],
        mom_new_b,
        upd_b.astype(jnp.bfloat16),
        out_b,
    )


def solution(mesh):
    fine = Mesh(mesh.devices.reshape(4, 8, 4, 2), ("x", "z", "y", "core"))
    spec = P(ROW, COL)
    return jax.shard_map(
        shards, mesh=fine, in_specs=(spec,) * 6, out_specs=(spec,) * 6, check_vma=False
    )
```
